256 devices in a mesh: kpt: 8 (over y, x_hi), row: 4 (over x_lo, core), col: 8 (over z).
Axes of the slice: x: 4 (x_hi: 2, x_lo: 2; x = x_hi * 2 + x_lo), y: 4, z: 8, core: 2. Of those that a mesh axis runs over, the one named last changes fastest.
Arguments:
- left_blocks: bfloat16 [32, 64, 2, 2, 128, 128], P(('kpt', 'row'), 'col'), parts along dimension 0, may hold values from -0.5 to 0.5
- left_rows: int32 [32, 64, 2], P(('kpt', 'row'), 'col'), parts along dimension 0, may hold values from 0 to 7, as said below
- left_count: int32 [32, 64], P(('kpt', 'row'), 'col'), parts along dimension 0, may hold values from 1 to 2, as said below
- left_level: int32 [32, 64, 2], P(('kpt', 'row'), 'col'), parts along dimension 0, may hold values from 0 to 7
- right_blocks: bfloat16 [16, 32, 8, 2, 2, 128, 128], P('kpt', 'row', 'col'), parts along dimension 0, may hold values from -6 to 6
- right_cols: int32 [16, 32, 8, 2], P('kpt', 'row', 'col'), parts along dimension 0, may hold values from 0 to 7, as said below
- right_count: int32 [16, 32, 8], P('kpt', 'row', 'col'), parts along dimension 0, may hold values from 1 to 2, as said below
- right_level: int32 [16, 32, 8, 2], P('kpt', 'row', 'col'), parts along dimension 0, may hold values from 0 to 7
Outputs:
- product_blocks: bfloat16 [256, 64, 2, 128, 128], P(('kpt', 'row'), 'col'), parts along dimension 0
The draws below stay inside these ranges and needn't reach their ends.
There are 8 independent parts, one for each index of `kpt`. The reference program is written for one: setup_inputs(seed, part) draws one part's arguments, and reference() takes and returns one part's arrays. A program takes and returns all parts, laid end to end along the dimension named above; each array names one. Nothing has to cross between parts.
Inputs may be any that keep to these rules, and one draw needn't show every extreme that they name: `left_rows`: the 2 slots of one row group and block column name distinct block rows. `left_count`: in every row group some block column has all 2 slots live. `right_cols`: the 2 slots of one block row and column group name distinct block columns. `right_count`: in every column group some block row has all 2 slots live.
All inputs are finite; a program needn't handle non-finite values.
Results may differ from the reference program's by a relative error of at most 0.001.
Values may be sent and summed in bfloat16 or wider, within the bound.
No kernel may reach another device: no remote copies, remote signals or barrier semaphores. Data moves between devices by JAX's collectives and lax.ppermute only.
A program may use at most 192 MiB of HBM per device.

```python
import jax
import jax.numpy as jnp
from jax import lax

BS = 128
GR = 8
LEVEL_CUT = 7
NB = 64
KB = 8
MA = 2
MB = 2
SETS = 2
N_ROW = 4
N_COL = 8


def distinct_slots(key, count, choices, taken):
    keys = jax.random.split(key, count)
    orders = jax.vmap(lambda single: jax.random.permutation(single, choices))(keys)
    return orders[:, :taken].astype(jnp.int32)


def filled_counts(key, groups, length, most):
    base = jax.random.randint(jax.random.fold_in(key, 1), (groups, length), 1, most + 1)
    chosen = jax.random.randint(jax.random.fold_in(key, 2), (groups, 1), 0, length)
    position = jnp.arange(length, dtype=jnp.int32)[None, :]
    return jnp.where(position == chosen, most, base).astype(jnp.int32)


def draw_left_rows(key, part):
    slots = distinct_slots(jax.random.fold_in(key, 101), N_ROW * NB, GR, MA)
    return slots.reshape(N_ROW, NB, MA)


def draw_left_count(key, part):
    return filled_counts(jax.random.fold_in(key, 202), N_ROW, NB, MA)


def draw_right_cols(key, part):
    slots = distinct_slots(jax.random.fold_in(key, 303), NB * N_COL, KB, MB)
    return slots.reshape(N_COL // N_ROW, N_ROW * KB, N_COL, MB)


def draw_right_count(key, part):
    counts = filled_counts(jax.random.fold_in(key, 404), N_COL, NB, MB)
    return counts.T.reshape(N_COL // N_ROW, N_ROW * KB, N_COL)


def set_ends(array, key, low, top_value):
    longest = array.shape.index(max(array.shape))
    spots = []
    for shift in (0, 1):
        where = [jax.random.randint(jax.random.fold_in(key, axis), (), 0, length) for axis, length in enumerate(array.shape)]
        where[longest] = (where[longest] + shift) % array.shape[longest]
        spots.append(tuple(where))
    return array.at[spots[0]].set(low).at[spots[1]].set(top_value)


def shard_levels(rng, dims, cuts, least, high):
    factor_of, own = 1.0, jax.random.fold_in(rng, 6)
    for axis_at, parts in cuts:
        steps = jnp.exp(jax.random.uniform(jax.random.fold_in(own, axis_at), (parts,), jnp.float32, least / len(cuts), high / len(cuts)))
        factor_of = factor_of * jnp.repeat(steps, dims[axis_at] // parts).reshape([-1 if axis == axis_at else 1 for axis in range(len(dims))])
    return factor_of


def gaussian(rng, shape, width, limit, pieces=(), kind=jnp.bfloat16):
    values = jax.random.normal(rng, shape, jnp.float32) * width
    if len(pieces) > 0:
        values = shard_levels(rng, shape, pieces, -0.22, 0.18) * values
    return jnp.clip(values, min=-limit, max=limit).astype(kind)


def setup_inputs(seed: int = 0, part: int = 0) -> dict:
    key_list = jax.random.split(jax.random.key(seed), 9)
    own_keys = jax.random.split(jax.random.fold_in(key_list[8], part), 9)
    left_blocks = gaussian(own_keys[0], (N_ROW, NB, MA, 2, BS, BS), BS ** -0.5, 0.5, ((0, 4), (1, 8)))
    left_rows = draw_left_rows(jax.random.fold_in(jax.random.fold_in(key_list[8], part), 71), part)
    left_count = draw_left_count(jax.random.fold_in(jax.random.fold_in(key_list[8], part), 71), part)
    left_level = set_ends(jax.random.randint(own_keys[3], (N_ROW, NB, MA), 0, 8), jax.random.fold_in(own_keys[3], 1), 0, 7).astype(jnp.int32)
    right_blocks = gaussian(own_keys[4], (SETS, N_ROW * KB, N_COL, MB, 2, BS, BS), 1.0, 6.0, ((1, 4), (2, 8)))
    right_cols = draw_right_cols(jax.random.fold_in(jax.random.fold_in(key_list[8], part), 71), part)
    right_count = draw_right_count(jax.random.fold_in(jax.random.fold_in(key_list[8], part), 71), part)
    right_level = set_ends(jax.random.randint(own_keys[7], (SETS, N_ROW * KB, N_COL, MB), 0, 8), jax.random.fold_in(own_keys[7], 1), 0, 7).astype(jnp.int32)
    return dict(left_blocks=left_blocks, left_rows=left_rows, left_count=left_count, left_level=left_level, right_blocks=right_blocks, right_cols=right_cols, right_count=right_count, right_level=right_level)


def reference(left_blocks, left_rows, left_count, left_level, right_blocks, right_cols, right_count, right_level):
    right_flat = right_blocks.reshape(NB, N_COL, MB, 2, BS, BS)
    cols_flat = right_cols.reshape(NB, N_COL, MB)
    count_flat = right_count.reshape(NB, N_COL)
    level_flat = right_level.reshape(NB, N_COL, MB)
    slot_left = jnp.arange(MA, dtype=jnp.int32)
    slot_right = jnp.arange(MB, dtype=jnp.int32)
    group_base = (jnp.arange(N_ROW, dtype=jnp.int32) * GR)[:, None, None, None]
    panel_base = (jnp.arange(N_COL, dtype=jnp.int32) * KB)[None, None, :, None]

    def one_column(total, column):
        blocks_a, rows_a, count_a, level_a, blocks_b, cols_b, count_b, level_b = column
        live_a = slot_left[None, :] < count_a.astype(jnp.int32)[:, None]
        live_b = slot_right[None, :] < count_b.astype(jnp.int32)[:, None]
        kept = live_a[:, :, None, None] & live_b[None, None, :, :]
        kept = kept & (level_a.astype(jnp.int32)[:, :, None, None] + level_b.astype(jnp.int32)[None, None, :, :] >= LEVEL_CUT)
        terms = jnp.einsum("pmcij,qndjl->pmqncdil", blocks_a.astype(jnp.float32), blocks_b.astype(jnp.float32),
                           precision=lax.Precision.HIGHEST)
        real_part = terms[:, :, :, :, 0, 0] - terms[:, :, :, :, 1, 1]
        imag_part = terms[:, :, :, :, 0, 1] + terms[:, :, :, :, 1, 0]
        product = jnp.stack([real_part, imag_part], axis=4) * kept[..., None, None, None].astype(jnp.float32)
        row_index = group_base + rows_a.astype(jnp.int32)[:, :, None, None]
        col_index = panel_base + cols_b.astype(jnp.int32)[None, None, :, :]
        row_index = jnp.broadcast_to(row_index, kept.shape).reshape(-1)
        col_index = jnp.broadcast_to(col_index, kept.shape).reshape(-1)
        total = total.at[row_index, col_index].add(product.reshape(-1, 2, BS, BS))
        return total, None

    columns = (jnp.moveaxis(left_blocks, 1, 0), jnp.moveaxis(left_rows, 1, 0), jnp.moveaxis(left_count, 1, 0),
               jnp.moveaxis(left_level, 1, 0), right_flat, cols_flat, count_flat, level_flat)
    total = jnp.zeros((N_ROW * GR, NB, 2, BS, BS), jnp.float32)
    total, unused = lax.scan(one_column, total, columns)
    return total.astype(jnp.bfloat16)
```

```python
import functools

import jax
import jax.numpy as jnp
from jax import lax
from jax.experimental import pallas as pl
from jax.experimental.pallas import tpu as pltpu
from jax.sharding import PartitionSpec as P

GR = 8
KB = 8
BS = 128
LEVEL_CUT = 7
HALF = 4
BLOCK_ROWS = 2 * 2 * BS
META = 16
CHUNK = HALF * BLOCK_ROWS
PANEL = KB * BLOCK_ROWS


def fill_table(table_ref, places, count, level, rows):
    lane = lax.broadcasted_iota(jnp.int32, (META, BS), 1)
    sub = lax.broadcasted_iota(jnp.int32, (META, BS), 0)
    table = jnp.zeros((META, BS), jnp.float32)
    for k in range(rows):
        for m in range(2):
            live = (m < count(k)).astype(jnp.int32)
            for at, value in ((m, places(k, m)), (2 + m, level(k, m)), (4 + m, live)):
                table = jnp.where((sub == k) & (lane == at), value.astype(jnp.float32), table)
    table_ref[...] = table.astype(jnp.bfloat16)


def pack_left_kernel(rows_ref, count_ref, level_ref, blocks_ref, first_ref, second_ref, sem):
    outs = (first_ref, second_ref)
    copies = [
        pltpu.make_async_copy(
            blocks_ref.at[pl.ds(h * CHUNK, CHUNK)], outs[h].at[pl.ds(0, CHUNK)], sem.at[h]
        )
        for h in range(2)
    ]
    for copy in copies:
        copy.start()
    for h in range(2):
        fill_table(
            outs[h].at[pl.ds(CHUNK, META)],
            lambda k, m: rows_ref[m, h * HALF + k],
            lambda k: count_ref[0, h * HALF + k],
            lambda k, m: level_ref[m, h * HALF + k],
            HALF,
        )
    for copy in copies:
        copy.wait()


def pack_left(blocks, rows, count, level):
    shape = pltpu.VMEM((CHUNK + META, BS), jnp.bfloat16)
    return pl.pallas_call(
        pack_left_kernel,
        out_shape=(shape, shape),
        in_specs=[pl.BlockSpec(memory_space=pltpu.SMEM)] * 3
        + [pl.BlockSpec(memory_space=pltpu.HBM)],
        out_specs=[pl.BlockSpec(memory_space=pltpu.VMEM)] * 2,
        scratch_shapes=[pltpu.SemaphoreType.DMA((2,))],
    )(jnp.swapaxes(rows[0], 0, 1), count, jnp.swapaxes(level[0], 0, 1), blocks.reshape(-1, BS))


def pack_right_kernel(which_ref, cols_ref, count_ref, level_ref, blocks_ref, out_ref, sem):
    which = which_ref[0]
    blocks = pltpu.make_async_copy(blocks_ref.at[which], out_ref.at[pl.ds(0, PANEL)], sem)
    blocks.start()
    fill_table(
        out_ref.at[pl.ds(PANEL, META)],
        lambda k, m: cols_ref[which, m, k],
        lambda k: count_ref[which, 0, k],
        lambda k, m: level_ref[which, m, k],
        KB,
    )
    blocks.wait()


def pack_right(which, blocks, cols, count, level):
    return pl.pallas_call(
        pack_right_kernel,
        out_shape=pltpu.VMEM((PANEL + META, BS), jnp.bfloat16),
        in_specs=[pl.BlockSpec(memory_space=pltpu.SMEM)] * 4
        + [pl.BlockSpec(memory_space=pltpu.HBM)],
        out_specs=pl.BlockSpec(memory_space=pltpu.VMEM),
        scratch_shapes=[pltpu.SemaphoreType.DMA],
    )(
        which,
        jnp.swapaxes(cols[:, :, 0], 1, 2),
        jnp.swapaxes(count, 1, 2),
        jnp.swapaxes(level[:, :, 0], 1, 2),
        blocks.reshape(-1, PANEL, BS),
    )


def shifted(value, axis, steps):
    count = lax.axis_size(axis)
    return lax.ppermute(value, axis, [(i, (i + steps) % count) for i in range(count)])


def crossed(value, axis, bit):
    count = lax.axis_size(axis)
    return lax.ppermute(value, axis, [(i, i ^ bit) for i in range(count)])


def multiply_kernel(offsets, halves, first, last, grid_rows, grid_cols, n_rights, *refs):
    n = len(offsets)
    where_ref = refs[0]
    lefts = refs[1 : 1 + n]
    rights = refs[1 + n : 1 + n + n_rights]
    rest = refs[1 + n + n_rights :]
    if not first:
        acc_ref = rest[0]
        rest = rest[1:]
    out_ref = rest[0]
    rest = rest[1:]
    if last:
        stage_ref = rest[0]
        rest = rest[1:]
    else:
        acc_ref = out_ref
    left_buf, right_buf, table_buf, whole_buf, table_smem, data_sem, table_sem, smem_sem, out_sem = rest
    own_row = where_ref[0]
    own_col = where_ref[1]

    def right_copies(i, act):
        panel = (own_col + offsets[i] + grid_cols) % grid_cols
        source = (panel % grid_rows) ^ own_row
        near = -1 <= offsets[i] <= grid_rows - 2
        for s in range(grid_rows):

            @pl.when(source == s)
            def _(s=s):
                act(rights[s if near else n_rights - grid_rows + s])

    for i in range(n):
        pltpu.make_async_copy(
            lefts[i].at[pl.ds(CHUNK, META)], table_buf.at[2 * i], table_sem
        ).start()
        right_copies(
            i,
            lambda src, i=i: pltpu.make_async_copy(
                src.at[pl.ds(PANEL, META)], table_buf.at[2 * i + 1], table_sem
            ).start(),
        )
    for i in range(n):
        pltpu.make_async_copy(lefts[i].at[pl.ds(0, CHUNK)], left_buf.at[i], data_sem.at[i]).start()
        right_copies(
            i,
            lambda src, i=i: pltpu.make_async_copy(
                src.at[pl.ds(halves[i] * CHUNK, CHUNK)], right_buf.at[i], data_sem.at[i]
            ).start(),
        )
    if first:
        acc_ref[...] = jnp.zeros_like(acc_ref)
    pltpu.make_async_copy(table_buf, table_buf, table_sem).wait()
    whole_buf[...] = table_buf[:, : whole_buf.shape[1]].astype(jnp.float32).astype(jnp.int32)
    to_smem = pltpu.make_async_copy(whole_buf, table_smem, smem_sem)
    to_smem.start()
    to_smem.wait()

    def one_item(i, half_kb):
        pltpu.make_async_copy(left_buf.at[i], left_buf.at[i], data_sem.at[i]).wait()
        pltpu.make_async_copy(right_buf.at[i], right_buf.at[i], data_sem.at[i]).wait()

        def one_kb(k, carry):
            kr = half_kb + k
            base = pl.multiple_of(k * BLOCK_ROWS, BLOCK_ROWS)

            def right_part(slot, part):
                return right_buf[i, pl.ds(base + (2 * slot + part) * BS, BS), :]

            right = jnp.concatenate(
                [
                    jnp.concatenate([right_part(0, 0), right_part(1, 0)], axis=1),
                    jnp.concatenate([right_part(0, 1), right_part(1, 1)], axis=1),
                ],
                axis=0,
            )
            for m in range(2):
                row = table_smem[2 * i, k, m]
                level = table_smem[2 * i, k, 2 + m]
                live = table_smem[2 * i, k, 4 + m] > 0
                kept = [
                    live
                    & (table_smem[2 * i + 1, kr, 4 + q] > 0)
                    & (level + table_smem[2 * i + 1, kr, 2 + q] >= LEVEL_CUT)
                    for q in range(2)
                ]

                @pl.when(kept[0] | kept[1])
                def _():
                    real = left_buf[i, pl.ds(base + 2 * m * BS, BS), :]
                    imag = left_buf[i, pl.ds(base + (2 * m + 1) * BS, BS), :]
                    left = jnp.concatenate(
                        [
                            jnp.concatenate([real, -imag], axis=1),
                            jnp.concatenate([imag, real], axis=1),
                        ],
                        axis=0,
                    )
                    product = jnp.dot(left, right, preferred_element_type=jnp.float32)
                    for q in range(2):

                        @pl.when(kept[q])
                        def _(q=q):
                            col = table_smem[2 * i + 1, kr, q]
                            for part in range(2):
                                acc_ref[row, col, part] += product[
                                    part * BS : (part + 1) * BS, q * BS : (q + 1) * BS
                                ]

            return carry

        lax.fori_loop(0, HALF, one_kb, 0)

    assert all(h == i % 2 for i, h in enumerate(halves))
    lax.fori_loop(0, n, lambda i, c: (one_item(i, (i % 2) * HALF), c)[1], 0)

    if last:
        for r in range(GR):
            stage_ref[r] = acc_ref[r].astype(jnp.bfloat16)
            pltpu.make_async_copy(stage_ref.at[r], out_ref.at[r], out_sem).start()
        pltpu.make_async_copy(stage_ref, out_ref, out_sem).wait()


def multiply(where, items, rights, total, last, local):
    grid_rows = lax.axis_size("row")
    grid_cols = lax.axis_size("col")
    lefts = [value for value, _, _ in items]
    offsets = tuple(offset for _, offset, _ in items)
    halves = tuple(half for _, _, half in items)
    n = len(items)
    first = total is None
    shape = (GR, KB, 2, BS, BS)
    operands = [where, *lefts, *rights]
    in_specs = [pl.BlockSpec(memory_space=pltpu.SMEM)]
    in_specs += [
        pl.BlockSpec(memory_space=pltpu.VMEM if any(v is own for own in local) else pltpu.HBM)
        for v in operands[1:]
    ]
    scratch = []
    aliases = {}
    if not first:
        operands.append(total)
        in_specs.append(pl.BlockSpec(memory_space=pltpu.VMEM))
    if last:
        out_shape = jax.ShapeDtypeStruct(shape, jnp.bfloat16)
        out_specs = pl.BlockSpec(memory_space=pltpu.HBM)
        scratch = [pltpu.VMEM(shape, jnp.bfloat16)]
    else:
        out_shape = pltpu.VMEM(shape, jnp.float32)
        out_specs = pl.BlockSpec(memory_space=pltpu.VMEM)
        if not first:
            aliases = {len(operands) - 1: 0}
    scratch += [
        pltpu.VMEM((n, CHUNK, BS), jnp.bfloat16),
        pltpu.VMEM((n, CHUNK, BS), jnp.bfloat16),
        pltpu.VMEM((2 * n, META, BS), jnp.bfloat16),
        pltpu.VMEM((2 * n, KB, BS), jnp.int32),
        pltpu.SMEM((2 * n, KB, BS), jnp.int32),
        pltpu.SemaphoreType.DMA((n,)),
        pltpu.SemaphoreType.DMA,
        pltpu.SemaphoreType.DMA,
        pltpu.SemaphoreType.DMA,
    ]
    kernel = functools.partial(
        multiply_kernel, offsets, halves, first, last, grid_rows, grid_cols, len(rights)
    )
    return pl.pallas_call(
        kernel,
        out_shape=out_shape,
        in_specs=in_specs,
        out_specs=out_specs,
        scratch_shapes=scratch,
        input_output_aliases=aliases,
        compiler_params=pltpu.CompilerParams(vmem_limit_bytes=32 * 1024 * 1024),
    )(*operands)


def body(
    left_blocks,
    left_rows,
    left_count,
    left_level,
    right_blocks,
    right_cols,
    right_count,
    right_level,
):
    row, col = lax.axis_index("row"), lax.axis_index("col")
    grid_rows, grid_cols = lax.axis_size("row"), lax.axis_size("col")
    start = col + grid_cols - 1
    near = (((start + (row - start) % grid_rows) % grid_cols) // grid_rows).astype(jnp.int32)
    where = jnp.stack([row, col]).astype(jnp.int32)
    own = list(pack_left(left_blocks, left_rows, left_count, left_level))
    right = (right_blocks, right_cols, right_count, right_level)
    held = [pack_right(which.reshape(1), *right) for which in (near, 1 - near)]

    hops = []
    up, down = list(own), list(own)
    for step in range(1, 4):
        for h in range(2):
            up[h] = shifted(up[h], "col", 1)
            down[h] = shifted(down[h], "col", -1)
        hops.append(
            [(up[0], -step, 0), (up[1], -step, 1), (down[0], step, 0), (down[1], step, 1)]
        )
    hops.append([(shifted(up[0], "col", 1), -4, 0), (shifted(down[1], "col", -1), 4, 1)])
    rights = []
    for s in range(2):
        partner = crossed(held[s], "row", 1)
        other = crossed(held[s], "row", 2)
        corner = crossed(other, "row", 1)
        rights += [held[s], partner, other, corner]

    local = own + held
    own_items = [(own[0], 0, 0), (own[1], 0, 1)]
    total = multiply(where, own_items + hops[0], rights[:4], None, False, local)
    total = multiply(where, hops[1], rights, total, False, local)
    total = multiply(where, hops[2], rights[4:], total, False, local)
    return multiply(where, hops[3], rights[4:], total, True, local)


def solution(mesh):
    in_specs = (
        P(("kpt", "row"), "col", None, None, None, None),
        P(("kpt", "row"), "col", None),
        P(("kpt", "row"), "col"),
        P(("kpt", "row"), "col", None),
        P("kpt", "row", "col", None, None, None, None),
        P("kpt", "row", "col", None),
        P("kpt", "row", "col"),
        P("kpt", "row", "col", None),
    )
    out_specs = P(("kpt", "row"), "col", None, None, None)

    return jax.shard_map(body, mesh=mesh, in_specs=in_specs, out_specs=out_specs, check_vma=False)
```

```python
import functools

import jax
import jax.numpy as jnp
from jax import lax
from jax.experimental import pallas as pl
from jax.experimental.pallas import tpu as pltpu
from jax.sharding import PartitionSpec as P

GR = 8
KB = 8
BS = 128
LEVEL_CUT = 7
HALF = 4
BLOCK_ROWS = 2 * 2 * BS
META = 16
UNROLL = 4
MIB = 1024 * 1024
PACK_LIMIT = (60, 2)
CHUNK = HALF * BLOCK_ROWS
PANEL = KB * BLOCK_ROWS


def fill_table(table_ref, places, count, level, rows):
    lane = lax.broadcasted_iota(jnp.int32, (META, BS), 1)
    sub = lax.broadcasted_iota(jnp.int32, (META, BS), 0)
    table = jnp.zeros((META, BS), jnp.float32)
    for k in range(rows):
        for m in range(2):
            live = (m < count(k)).astype(jnp.int32)
            for at, value in ((m, places(k, m)), (2 + m, level(k, m)), (4 + m, live)):
                table = jnp.where((sub == k) & (lane == at), value.astype(jnp.float32), table)
    table_ref[...] = table.astype(jnp.bfloat16)


def pack_left_kernel(
    half, rows_hbm, count_hbm, level_hbm, blocks_ref, out_ref, rows_ref, count_ref, level_ref, sem
):
    copies = [
        pltpu.make_async_copy(source, target, sem.at[i])
        for i, (source, target) in enumerate(
            (
                (rows_hbm, rows_ref),
                (count_hbm, count_ref),
                (level_hbm, level_ref),
                (blocks_ref.at[pl.ds(half * CHUNK, CHUNK)], out_ref.at[pl.ds(0, CHUNK)]),
            )
        )
    ]
    for copy in copies:
        copy.start()
    for copy in copies[:3]:
        copy.wait()
    fill_table(
        out_ref.at[pl.ds(CHUNK, META)],
        lambda k, m: rows_ref[m, half * HALF + k],
        lambda k: count_ref[0, half * HALF + k],
        lambda k, m: level_ref[m, half * HALF + k],
        HALF,
    )
    copies[3].wait()


def pack_left(half, blocks, rows, count, level):
    tables = (jnp.swapaxes(rows[0], 0, 1), count, jnp.swapaxes(level[0], 0, 1))
    return pl.pallas_call(
        functools.partial(pack_left_kernel, half),
        out_shape=pltpu.VMEM((CHUNK + META, BS), jnp.bfloat16),
        in_specs=[pl.BlockSpec(memory_space=pltpu.HBM)] * 4,
        out_specs=pl.BlockSpec(memory_space=pltpu.VMEM),
        scratch_shapes=[pltpu.SMEM(table.shape, jnp.int32) for table in tables]
        + [pltpu.SemaphoreType.DMA((4,))],
        compiler_params=pltpu.CompilerParams(vmem_limit_bytes=PACK_LIMIT[half] * MIB),
    )(*tables, blocks.reshape(-1, BS))


def pack_right_kernel(which_ref, cols_ref, count_ref, level_ref, blocks_ref, out_ref, sem):
    which = which_ref[0]
    blocks = pltpu.make_async_copy(blocks_ref.at[which], out_ref.at[pl.ds(0, PANEL)], sem)
    blocks.start()
    fill_table(
        out_ref.at[pl.ds(PANEL, META)],
        lambda k, m: cols_ref[which, m, k],
        lambda k: count_ref[which, 0, k],
        lambda k, m: level_ref[which, m, k],
        KB,
    )
    blocks.wait()


def pack_right(which, blocks, cols, count, level):
    return pl.pallas_call(
        pack_right_kernel,
        out_shape=pltpu.VMEM((PANEL + META, BS), jnp.bfloat16),
        in_specs=[pl.BlockSpec(memory_space=pltpu.SMEM)] * 4
        + [pl.BlockSpec(memory_space=pltpu.HBM)],
        out_specs=pl.BlockSpec(memory_space=pltpu.VMEM),
        scratch_shapes=[pltpu.SemaphoreType.DMA],
        compiler_params=pltpu.CompilerParams(vmem_limit_bytes=2 * MIB),
    )(
        which,
        jnp.swapaxes(cols[:, :, 0], 1, 2),
        jnp.swapaxes(count, 1, 2),
        jnp.swapaxes(level[:, :, 0], 1, 2),
        blocks.reshape(-1, PANEL, BS),
    )


def shifted(value, axis, steps):
    count = lax.axis_size(axis)
    return lax.ppermute(value, axis, [(i, (i + steps) % count) for i in range(count)])


def crossed(value, axis, bit):
    count = lax.axis_size(axis)
    return lax.ppermute(value, axis, [(i, i ^ bit) for i in range(count)])


def kept_pairs(table_smem, left_at, right_at, k, kr, m):
    level = table_smem[left_at, k, 2 + m]
    live = table_smem[left_at, k, 4 + m] > 0
    return [
        live
        & (table_smem[right_at, kr, 4 + q] > 0)
        & (level + table_smem[right_at, kr, 2 + q] >= LEVEL_CUT)
        for q in range(2)
    ]


def add_products(acc_ref, table_smem, left_at, right_at, k, kr, left_part, right_part, mark):
    right = jnp.concatenate(
        [
            jnp.concatenate([right_part(0, 0), right_part(1, 0)], axis=1),
            jnp.concatenate([right_part(0, 1), right_part(1, 1)], axis=1),
        ],
        axis=0,
    )
    for m in range(2):
        row = table_smem[left_at, k, m]
        kept = kept_pairs(table_smem, left_at, right_at, k, kr, m)
        real, imag = left_part(m, 0), left_part(m, 1)
        left = jnp.concatenate(
            [
                jnp.concatenate([real, -imag], axis=1),
                jnp.concatenate([imag, real], axis=1),
            ],
            axis=0,
        )
        product = jnp.dot(left, right, preferred_element_type=jnp.float32)
        for q in range(2):
            col = table_smem[right_at, kr, q]
            weight = kept[q].astype(jnp.float32)
            for part in range(2):
                acc_ref[row, col, part] += weight * product[
                    part * BS : (part + 1) * BS, q * BS : (q + 1) * BS
                ]
            mark(kept[q], row, col)


def tables_to_smem(table_buf, whole_buf, table_smem, sem):
    whole_buf[...] = table_buf[:, : whole_buf.shape[1]].astype(jnp.float32).astype(jnp.int32)
    to_smem = pltpu.make_async_copy(whole_buf, table_smem, sem)
    to_smem.start()
    to_smem.wait()


def right_source(where_ref, offset, grid_rows, grid_cols):
    panel = (where_ref[1] + offset + grid_cols) % grid_cols
    return (panel % grid_rows) ^ where_ref[0]


def multiply_kernel(offsets, halves, first, grid_rows, grid_cols, n_rights, *refs):
    n = len(offsets)
    where_ref = refs[0]
    lefts = refs[1 : 1 + n]
    rights = refs[1 + n : 1 + n + n_rights]
    acc_ref = refs[1 + n + n_rights + (not first)]
    left_buf, right_buf, table_buf, whole_buf, table_smem, data_sem, table_sem, smem_sem = refs[
        2 + n + n_rights + (not first) :
    ]

    def right_copies(i, act):
        source = right_source(where_ref, offsets[i], grid_rows, grid_cols)
        near = -1 <= offsets[i] <= grid_rows - 2
        for s in range(grid_rows):

            @pl.when(source == s)
            def _(s=s):
                act(rights[s if near else n_rights - grid_rows + s])

    for i in range(n):
        pltpu.make_async_copy(
            lefts[i].at[pl.ds(CHUNK, META)], table_buf.at[2 * i], table_sem
        ).start()
        right_copies(
            i,
            lambda src, i=i: pltpu.make_async_copy(
                src.at[pl.ds(PANEL, META)], table_buf.at[2 * i + 1], table_sem
            ).start(),
        )
    for i in range(n):
        pltpu.make_async_copy(lefts[i].at[pl.ds(0, CHUNK)], left_buf.at[i], data_sem.at[i]).start()
        right_copies(
            i,
            lambda src, i=i: pltpu.make_async_copy(
                src.at[pl.ds(halves[i] * CHUNK, CHUNK)], right_buf.at[i], data_sem.at[i]
            ).start(),
        )
    if first:
        acc_ref[...] = jnp.zeros_like(acc_ref)
    pltpu.make_async_copy(table_buf, table_buf, table_sem).wait()
    tables_to_smem(table_buf, whole_buf, table_smem, smem_sem)
    assert all(h == i % 2 for i, h in enumerate(halves))

    def one_item(i, carry):
        pltpu.make_async_copy(left_buf.at[i], left_buf.at[i], data_sem.at[i]).wait()
        pltpu.make_async_copy(right_buf.at[i], right_buf.at[i], data_sem.at[i]).wait()

        def one_kb(k, carry):
            base = pl.multiple_of(k * BLOCK_ROWS, BLOCK_ROWS)
            add_products(
                acc_ref,
                table_smem,
                2 * i,
                2 * i + 1,
                k,
                (i % 2) * HALF + k,
                lambda slot, part: left_buf[i, pl.ds(base + (2 * slot + part) * BS, BS), :],
                lambda slot, part: right_buf[i, pl.ds(base + (2 * slot + part) * BS, BS), :],
                lambda kept, row, col: None,
            )
            return carry

        return lax.fori_loop(0, HALF, one_kb, carry, unroll=UNROLL)

    lax.fori_loop(0, n, one_item, 0)


def fetch_kernel(offset, grid_rows, grid_cols, where_ref, *refs):
    *rights, out_ref, sem = refs
    source = right_source(where_ref, offset, grid_rows, grid_cols)
    for s in range(grid_rows):

        @pl.when(source == s)
        def _(s=s):
            pltpu.make_async_copy(rights[s], out_ref, sem).start()

    pltpu.make_async_copy(out_ref, out_ref, sem).wait()


def spaces(operands, local):
    return [
        pl.BlockSpec(memory_space=pltpu.VMEM if any(v is own for own in local) else pltpu.HBM)
        for v in operands
    ]


def fetch(where, offset, rights, local):
    kernel = functools.partial(
        fetch_kernel, offset, lax.axis_size("row"), lax.axis_size("col")
    )
    return pl.pallas_call(
        kernel,
        out_shape=pltpu.VMEM((PANEL + META, BS), jnp.bfloat16),
        in_specs=[pl.BlockSpec(memory_space=pltpu.SMEM)] + spaces(rights, local),
        out_specs=pl.BlockSpec(memory_space=pltpu.VMEM),
        scratch_shapes=[pltpu.SemaphoreType.DMA],
        compiler_params=pltpu.CompilerParams(vmem_limit_bytes=2 * MIB),
    )(where, *rights)


def flush_kernel(acc_ref, out_ref, stage_ref, sem):
    for r in range(GR):
        stage_ref[r] = acc_ref[r].astype(jnp.bfloat16)
        pltpu.make_async_copy(stage_ref.at[r], out_ref.at[r], sem).start()
    pltpu.make_async_copy(stage_ref, out_ref, sem).wait()


def flush(total):
    return pl.pallas_call(
        flush_kernel,
        out_shape=jax.ShapeDtypeStruct(total.shape, jnp.bfloat16),
        in_specs=[pl.BlockSpec(memory_space=pltpu.VMEM)],
        out_specs=pl.BlockSpec(memory_space=pltpu.HBM),
        scratch_shapes=[
            pltpu.VMEM(total.shape, jnp.bfloat16),
            pltpu.SemaphoreType.DMA,
        ],
        compiler_params=pltpu.CompilerParams(vmem_limit_bytes=6 * MIB),
    )(total)


def finish_kernel(
    up_ref, down_ref, right_ref, acc_ref, old_ref, out_ref,
    stage_ref, table_buf, whole_buf, table_smem, flag_smem, list_smem, out_sem, smem_sem,
):
    lefts = (up_ref, down_ref)
    for h in range(2):
        table_buf[h] = lefts[h][pl.ds(CHUNK, META), :]
    table_buf[2] = right_ref[pl.ds(PANEL, META), :]
    for at in range(GR * KB):
        flag_smem[at] = 0
    list_smem[GR * KB] = 0
    tables_to_smem(table_buf, whole_buf, table_smem, smem_sem)

    def mark(kept, row, col):
        at = row * KB + col

        @pl.when(kept & (flag_smem[at] == 0))
        def _():
            flag_smem[at] = 1
            count = list_smem[GR * KB]
            list_smem[count] = at
            list_smem[GR * KB] = count + 1

    for h in range(2):
        for k in range(HALF):
            for m in range(2):
                kept = kept_pairs(table_smem, h, 2, k, h * HALF + k, m)
                for q in range(2):
                    mark(kept[q], table_smem[h, k, m], table_smem[2, h * HALF + k, q])

    for h in range(2):

        def one_kb(k, carry, h=h):
            base = pl.multiple_of(k * BLOCK_ROWS, BLOCK_ROWS)
            add_products(
                acc_ref,
                table_smem,
                h,
                2,
                k,
                h * HALF + k,
                lambda slot, part: lefts[h][pl.ds(base + (2 * slot + part) * BS, BS), :],
                lambda slot, part: right_ref[
                    pl.ds(h * CHUNK + base + (2 * slot + part) * BS, BS), :
                ],
                lambda kept, row, col: None,
            )
            return carry

        lax.fori_loop(0, HALF, one_kb, 0, unroll=UNROLL)

    count = list_smem[GR * KB]

    def write_block(i, carry):
        at = list_smem[i]
        row, col = at // KB, at % KB
        stage_ref[i] = acc_ref[row, col].astype(jnp.bfloat16)
        pltpu.make_async_copy(stage_ref.at[i], out_ref.at[row, col], out_sem.at[i]).start()
        return carry

    def wait_block(i, carry):
        pltpu.make_async_copy(stage_ref.at[i], out_ref.at[0, 0], out_sem.at[i]).wait()
        return carry

    lax.fori_loop(0, count, write_block, 0)
    lax.fori_loop(0, count, wait_block, 0)


def finish(up, down, right, total, old):
    most = 2 * HALF * 4
    return pl.pallas_call(
        finish_kernel,
        out_shape=jax.ShapeDtypeStruct(old.shape, old.dtype),
        in_specs=[pl.BlockSpec(memory_space=pltpu.VMEM)] * 4
        + [pl.BlockSpec(memory_space=pltpu.HBM)],
        out_specs=pl.BlockSpec(memory_space=pltpu.HBM),
        input_output_aliases={4: 0},
        scratch_shapes=[
            pltpu.VMEM((most, 2, BS, BS), jnp.bfloat16),
            pltpu.VMEM((3, META, BS), jnp.bfloat16),
            pltpu.VMEM((3, KB, BS), jnp.int32),
            pltpu.SMEM((3, KB, BS), jnp.int32),
            pltpu.SMEM((GR * KB,), jnp.int32),
            pltpu.SMEM((GR * KB + 1,), jnp.int32),
            pltpu.SemaphoreType.DMA((most,)),
            pltpu.SemaphoreType.DMA,
        ],
        compiler_params=pltpu.CompilerParams(vmem_limit_bytes=5 * MIB),
    )(up, down, right, total, old)


def multiply(where, items, rights, total, local):
    grid_rows = lax.axis_size("row")
    grid_cols = lax.axis_size("col")
    lefts = [value for value, _, _ in items]
    offsets = tuple(offset for _, offset, _ in items)
    halves = tuple(half for _, _, half in items)
    n = len(items)
    first = total is None
    operands = [where, *lefts, *rights]
    in_specs = [pl.BlockSpec(memory_space=pltpu.SMEM)] + spaces(operands[1:], local)
    aliases = {}
    if not first:
        aliases = {len(operands): 0}
        operands.append(total)
        in_specs.append(pl.BlockSpec(memory_space=pltpu.VMEM))
    scratch = [
        pltpu.VMEM((n, CHUNK, BS), jnp.bfloat16),
        pltpu.VMEM((n, CHUNK, BS), jnp.bfloat16),
        pltpu.VMEM((2 * n, META, BS), jnp.bfloat16),
        pltpu.VMEM((2 * n, KB, BS), jnp.int32),
        pltpu.SMEM((2 * n, KB, BS), jnp.int32),
        pltpu.SemaphoreType.DMA((n,)),
        pltpu.SemaphoreType.DMA,
        pltpu.SemaphoreType.DMA,
    ]
    kernel = functools.partial(
        multiply_kernel, offsets, halves, first, grid_rows, grid_cols, len(rights)
    )
    return pl.pallas_call(
        kernel,
        out_shape=pltpu.VMEM((GR, KB, 2, BS, BS), jnp.float32),
        in_specs=in_specs,
        out_specs=pl.BlockSpec(memory_space=pltpu.VMEM),
        scratch_shapes=scratch,
        input_output_aliases=aliases,
        compiler_params=pltpu.CompilerParams(vmem_limit_bytes=16 * MIB),
    )(*operands)


def body(
    left_blocks,
    left_rows,
    left_count,
    left_level,
    right_blocks,
    right_cols,
    right_count,
    right_level,
):
    row, col = lax.axis_index("row"), lax.axis_index("col")
    grid_rows, grid_cols = lax.axis_size("row"), lax.axis_size("col")
    start = col + grid_cols - 1
    near = (((start + (row - start) % grid_rows) % grid_cols) // grid_rows).astype(jnp.int32)
    where = jnp.stack([row, col]).astype(jnp.int32)
    own = [pack_left(h, left_blocks, left_rows, left_count, left_level) for h in range(2)]
    right = (right_blocks, right_cols, right_count, right_level)
    held = [pack_right(which.reshape(1), *right) for which in (near, 1 - near)]

    hops = []
    up, down = list(own), list(own)
    for step in range(1, 4):
        for h in range(2):
            up[h] = shifted(up[h], "col", 1)
            down[h] = shifted(down[h], "col", -1)
        hops.append(
            [(up[0], -step, 0), (up[1], -step, 1), (down[0], step, 0), (down[1], step, 1)]
        )
    hops.append([(shifted(up[0], "col", 1), -4, 0), (shifted(down[1], "col", -1), 4, 1)])
    rights = []
    for s in range(2):
        partner = crossed(held[s], "row", 1)
        other = crossed(held[s], "row", 2)
        corner = crossed(other, "row", 1)
        rights += [held[s], partner, other, corner]

    local = own + held
    own_items = [(own[0], 0, 0), (own[1], 0, 1)]
    total = multiply(where, own_items + hops[0], rights[:4], None, local)
    total = multiply(where, hops[1], rights, total, local)
    last_right = fetch(where, 4, rights[4:], local)
    total = multiply(where, hops[2], rights[4:], total, local)
    early = flush(total)
    return finish(hops[3][0][0], hops[3][1][0], last_right, total, early)


def solution(mesh):
    in_specs = (
        P(("kpt", "row"), "col", None, None, None, None),
        P(("kpt", "row"), "col", None),
        P(("kpt", "row"), "col"),
        P(("kpt", "row"), "col", None),
        P("kpt", "row", "col", None, None, None, None),
        P("kpt", "row", "col", None),
        P("kpt", "row", "col"),
        P("kpt", "row", "col", None),
    )
    out_specs = P(("kpt", "row"), "col", None, None, None)

    return jax.shard_map(body, mesh=mesh, in_specs=in_specs, out_specs=out_specs, check_vma=False)
```

```python
import functools

import jax
import jax.numpy as jnp
from jax import lax
from jax.experimental import pallas as pl
from jax.experimental.pallas import tpu as pltpu
from jax.sharding import PartitionSpec as P

GR = 8
KB = 8
BS = 128
LEVEL_CUT = 7
HALF = 4
BLOCK_ROWS = 2 * 2 * BS
META = 16
UNROLL = 4
MIB = 1024 * 1024
PACK_LIMIT = (60, 2)
CHUNK = HALF * BLOCK_ROWS
PANEL = KB * BLOCK_ROWS


def fill_table(table_ref, places, count, level):
    slot = lax.broadcasted_iota(jnp.int32, places.shape, 0)
    rows = (places, level, (slot < count).astype(jnp.int32))
    table = jnp.concatenate([row.astype(jnp.float32) for row in rows], axis=0)
    table = jnp.pad(table, ((0, META - table.shape[0]), (0, BS - table.shape[1])))
    table_ref[...] = table.astype(jnp.bfloat16)


def pack_left_kernel(
    half, rows_hbm, count_hbm, level_hbm, blocks_ref, out_ref, rows_ref, count_ref, level_ref, sem
):
    blocks = pltpu.make_async_copy(
        blocks_ref.at[pl.ds(half * CHUNK, CHUNK)], out_ref.at[pl.ds(0, CHUNK)], sem.at[3]
    )
    copies = [
        pltpu.make_async_copy(source, target, sem.at[i])
        for i, (source, target) in enumerate(
            ((rows_hbm, rows_ref), (count_hbm, count_ref), (level_hbm, level_ref))
        )
    ]
    blocks.start()
    for copy in copies:
        copy.start()
    for copy in copies:
        copy.wait()
    fill_table(out_ref.at[pl.ds(CHUNK, META)], rows_ref[...], count_ref[...], level_ref[...])
    blocks.wait()


def pack_left(half, blocks, rows, count, level):
    tables = (jnp.swapaxes(rows[0], 0, 1), count, jnp.swapaxes(level[0], 0, 1))
    return pl.pallas_call(
        functools.partial(pack_left_kernel, half),
        out_shape=pltpu.VMEM((CHUNK + META, BS), jnp.bfloat16),
        in_specs=[pl.BlockSpec(memory_space=pltpu.HBM)] * 4,
        out_specs=pl.BlockSpec(memory_space=pltpu.VMEM),
        scratch_shapes=[pltpu.VMEM(table.shape, jnp.int32) for table in tables]
        + [pltpu.SemaphoreType.DMA((4,))],
        compiler_params=pltpu.CompilerParams(vmem_limit_bytes=PACK_LIMIT[half] * MIB),
    )(*tables, blocks.reshape(-1, BS))


def pack_right_kernel(
    which_ref, cols_hbm, count_hbm, level_hbm, blocks_ref, out_ref,
    cols_ref, count_ref, level_ref, sem,
):
    which = which_ref[0]
    blocks = pltpu.make_async_copy(
        blocks_ref.at[which], out_ref.at[pl.ds(0, PANEL)], sem.at[3]
    )
    copies = [
        pltpu.make_async_copy(source.at[which], target, sem.at[i])
        for i, (source, target) in enumerate(
            ((cols_hbm, cols_ref), (count_hbm, count_ref), (level_hbm, level_ref))
        )
    ]
    blocks.start()
    for copy in copies:
        copy.start()
    for copy in copies:
        copy.wait()
    fill_table(out_ref.at[pl.ds(PANEL, META)], cols_ref[...], count_ref[...], level_ref[...])
    blocks.wait()


def pack_right(which, blocks, cols, count, level):
    tables = (
        jnp.swapaxes(cols[:, :, 0], 1, 2),
        jnp.swapaxes(count, 1, 2),
        jnp.swapaxes(level[:, :, 0], 1, 2),
    )
    return pl.pallas_call(
        pack_right_kernel,
        out_shape=pltpu.VMEM((PANEL + META, BS), jnp.bfloat16),
        in_specs=[pl.BlockSpec(memory_space=pltpu.SMEM)]
        + [pl.BlockSpec(memory_space=pltpu.HBM)] * 4,
        out_specs=pl.BlockSpec(memory_space=pltpu.VMEM),
        scratch_shapes=[pltpu.VMEM(table.shape[1:], jnp.int32) for table in tables]
        + [pltpu.SemaphoreType.DMA((4,))],
        compiler_params=pltpu.CompilerParams(vmem_limit_bytes=2 * MIB),
    )(which, *tables, blocks.reshape(-1, PANEL, BS))


def shifted(value, axis, steps):
    count = lax.axis_size(axis)
    return lax.ppermute(value, axis, [(i, (i + steps) % count) for i in range(count)])


def crossed(value, axis, bit):
    count = lax.axis_size(axis)
    return lax.ppermute(value, axis, [(i, i ^ bit) for i in range(count)])


def kept_pairs(table_smem, left_at, right_at, kb, m):
    level = table_smem[left_at, 2 + m, kb]
    live = table_smem[left_at, 4 + m, kb] > 0
    return [
        live
        & (table_smem[right_at, 4 + q, kb] > 0)
        & (level + table_smem[right_at, 2 + q, kb] >= LEVEL_CUT)
        for q in range(2)
    ]


def add_products(acc_ref, table_smem, left_at, right_at, kb, left_part, right_part):
    right = jnp.concatenate(
        [
            jnp.concatenate([right_part(0, 0), right_part(1, 0)], axis=1),
            jnp.concatenate([right_part(0, 1), right_part(1, 1)], axis=1),
        ],
        axis=0,
    )
    for m in range(2):
        row = table_smem[left_at, m, kb]
        kept = kept_pairs(table_smem, left_at, right_at, kb, m)
        real, imag = left_part(m, 0), left_part(m, 1)
        left = jnp.concatenate(
            [
                jnp.concatenate([real, -imag], axis=1),
                jnp.concatenate([imag, real], axis=1),
            ],
            axis=0,
        )
        product = jnp.dot(left, right, preferred_element_type=jnp.float32)
        for q in range(2):
            col = table_smem[right_at, q, kb]
            weight = kept[q].astype(jnp.float32)
            for part in range(2):
                acc_ref[row, col, part] += weight * product[
                    part * BS : (part + 1) * BS, q * BS : (q + 1) * BS
                ]


def tables_to_smem(table_buf, whole_buf, table_smem, sem):
    whole_buf[...] = table_buf[:, : whole_buf.shape[1]].astype(jnp.float32).astype(jnp.int32)
    to_smem = pltpu.make_async_copy(whole_buf, table_smem, sem)
    to_smem.start()
    to_smem.wait()


def right_source(where_ref, offset, grid_rows, grid_cols):
    panel = (where_ref[1] + offset + grid_cols) % grid_cols
    return (panel % grid_rows) ^ where_ref[0]


def multiply_kernel(offsets, halves, first, grid_rows, grid_cols, n_rights, *refs):
    n = len(offsets)
    where_ref = refs[0]
    lefts = refs[1 : 1 + n]
    rights = refs[1 + n : 1 + n + n_rights]
    acc_ref = refs[1 + n + n_rights + (not first)]
    left_buf, right_buf, table_buf, whole_buf, table_smem, data_sem, table_sem, smem_sem = refs[
        2 + n + n_rights + (not first) :
    ]

    def right_copies(i, act):
        source = right_source(where_ref, offsets[i], grid_rows, grid_cols)
        near = -1 <= offsets[i] <= grid_rows - 2
        for s in range(grid_rows):

            @pl.when(source == s)
            def _(s=s):
                act(rights[s if near else n_rights - grid_rows + s])

    for i in range(n):
        pltpu.make_async_copy(
            lefts[i].at[pl.ds(CHUNK, META)], table_buf.at[2 * i], table_sem
        ).start()
        right_copies(
            i,
            lambda src, i=i: pltpu.make_async_copy(
                src.at[pl.ds(PANEL, META)], table_buf.at[2 * i + 1], table_sem
            ).start(),
        )
    for i in range(n):
        pltpu.make_async_copy(lefts[i].at[pl.ds(0, CHUNK)], left_buf.at[i], data_sem.at[i]).start()
        right_copies(
            i,
            lambda src, i=i: pltpu.make_async_copy(
                src.at[pl.ds(halves[i] * CHUNK, CHUNK)], right_buf.at[i], data_sem.at[i]
            ).start(),
        )
    if first:
        acc_ref[...] = jnp.zeros_like(acc_ref)
    pltpu.make_async_copy(table_buf, table_buf, table_sem).wait()
    tables_to_smem(table_buf, whole_buf, table_smem, smem_sem)
    assert all(h == i % 2 for i, h in enumerate(halves))

    def one_item(i, carry):
        pltpu.make_async_copy(left_buf.at[i], left_buf.at[i], data_sem.at[i]).wait()
        pltpu.make_async_copy(right_buf.at[i], right_buf.at[i], data_sem.at[i]).wait()

        def one_kb(k, carry):
            base = pl.multiple_of(k * BLOCK_ROWS, BLOCK_ROWS)
            add_products(
                acc_ref,
                table_smem,
                2 * i,
                2 * i + 1,
                (i % 2) * HALF + k,
                lambda slot, part: left_buf[i, pl.ds(base + (2 * slot + part) * BS, BS), :],
                lambda slot, part: right_buf[i, pl.ds(base + (2 * slot + part) * BS, BS), :],
            )
            return carry

        return lax.fori_loop(0, HALF, one_kb, carry, unroll=UNROLL)

    lax.fori_loop(0, n, one_item, 0)


def fetch_kernel(offset, grid_rows, grid_cols, where_ref, *refs):
    *rights, out_ref, sem = refs
    source = right_source(where_ref, offset, grid_rows, grid_cols)
    for s in range(grid_rows):

        @pl.when(source == s)
        def _(s=s):
            pltpu.make_async_copy(rights[s], out_ref, sem).start()

    pltpu.make_async_copy(out_ref, out_ref, sem).wait()


def spaces(operands, local):
    return [
        pl.BlockSpec(memory_space=pltpu.VMEM if any(v is own for own in local) else pltpu.HBM)
        for v in operands
    ]


def fetch(where, offset, rights, local):
    kernel = functools.partial(
        fetch_kernel, offset, lax.axis_size("row"), lax.axis_size("col")
    )
    return pl.pallas_call(
        kernel,
        out_shape=pltpu.VMEM((PANEL + META, BS), jnp.bfloat16),
        in_specs=[pl.BlockSpec(memory_space=pltpu.SMEM)] + spaces(rights, local),
        out_specs=pl.BlockSpec(memory_space=pltpu.VMEM),
        scratch_shapes=[pltpu.SemaphoreType.DMA],
        compiler_params=pltpu.CompilerParams(vmem_limit_bytes=2 * MIB),
    )(where, *rights)


def flush_kernel(acc_ref, out_ref, stage_ref, sem):
    for r in range(GR):
        stage_ref[r] = acc_ref[r].astype(jnp.bfloat16)
        pltpu.make_async_copy(stage_ref.at[r], out_ref.at[r], sem).start()
    pltpu.make_async_copy(stage_ref, out_ref, sem).wait()


def flush(total):
    return pl.pallas_call(
        flush_kernel,
        out_shape=jax.ShapeDtypeStruct(total.shape, jnp.bfloat16),
        in_specs=[pl.BlockSpec(memory_space=pltpu.VMEM)],
        out_specs=pl.BlockSpec(memory_space=pltpu.HBM),
        scratch_shapes=[
            pltpu.VMEM(total.shape, jnp.bfloat16),
            pltpu.SemaphoreType.DMA,
        ],
        compiler_params=pltpu.CompilerParams(vmem_limit_bytes=6 * MIB),
    )(total)


def finish_kernel(
    up_ref, down_ref, right_ref, acc_ref, old_ref, out_ref,
    stage_ref, table_buf, whole_buf, table_smem, flag_smem, list_smem, out_sem, smem_sem,
):
    lefts = (up_ref, down_ref)
    for h in range(2):
        table_buf[h] = lefts[h][pl.ds(CHUNK, META), :]
    table_buf[2] = right_ref[pl.ds(PANEL, META), :]
    for at in range(GR * KB):
        flag_smem[at] = 0
    list_smem[GR * KB] = 0
    tables_to_smem(table_buf, whole_buf, table_smem, smem_sem)

    def mark(kept, row, col):
        at = row * KB + col

        @pl.when(kept & (flag_smem[at] == 0))
        def _():
            flag_smem[at] = 1
            count = list_smem[GR * KB]
            list_smem[count] = at
            list_smem[GR * KB] = count + 1

    for h in range(2):
        for kb in range(h * HALF, (h + 1) * HALF):
            for m in range(2):
                kept = kept_pairs(table_smem, h, 2, kb, m)
                for q in range(2):
                    mark(kept[q], table_smem[h, m, kb], table_smem[2, q, kb])

    for h in range(2):

        def one_kb(k, carry, h=h):
            base = pl.multiple_of(k * BLOCK_ROWS, BLOCK_ROWS)
            add_products(
                acc_ref,
                table_smem,
                h,
                2,
                h * HALF + k,
                lambda slot, part: lefts[h][pl.ds(base + (2 * slot + part) * BS, BS), :],
                lambda slot, part: right_ref[
                    pl.ds(h * CHUNK + base + (2 * slot + part) * BS, BS), :
                ],
            )
            return carry

        lax.fori_loop(0, HALF, one_kb, 0, unroll=UNROLL)

    count = list_smem[GR * KB]

    def write_block(i, carry):
        at = list_smem[i]
        row, col = at // KB, at % KB
        stage_ref[i] = acc_ref[row, col].astype(jnp.bfloat16)
        pltpu.make_async_copy(stage_ref.at[i], out_ref.at[row, col], out_sem.at[i]).start()
        return carry

    def wait_block(i, carry):
        pltpu.make_async_copy(stage_ref.at[i], out_ref.at[0, 0], out_sem.at[i]).wait()
        return carry

    lax.fori_loop(0, count, write_block, 0)
    lax.fori_loop(0, count, wait_block, 0)


def finish(up, down, right, total, old):
    most = 2 * HALF * 4
    return pl.pallas_call(
        finish_kernel,
        out_shape=jax.ShapeDtypeStruct(old.shape, old.dtype),
        in_specs=[pl.BlockSpec(memory_space=pltpu.VMEM)] * 4
        + [pl.BlockSpec(memory_space=pltpu.HBM)],
        out_specs=pl.BlockSpec(memory_space=pltpu.HBM),
        input_output_aliases={4: 0},
        scratch_shapes=[
            pltpu.VMEM((most, 2, BS, BS), jnp.bfloat16),
            pltpu.VMEM((3, META, BS), jnp.bfloat16),
            pltpu.VMEM((3, KB, BS), jnp.int32),
            pltpu.SMEM((3, KB, BS), jnp.int32),
            pltpu.SMEM((GR * KB,), jnp.int32),
            pltpu.SMEM((GR * KB + 1,), jnp.int32),
            pltpu.SemaphoreType.DMA((most,)),
            pltpu.SemaphoreType.DMA,
        ],
        compiler_params=pltpu.CompilerParams(vmem_limit_bytes=5 * MIB),
    )(up, down, right, total, old)


def multiply(where, items, rights, total, local):
    grid_rows = lax.axis_size("row")
    grid_cols = lax.axis_size("col")
    lefts = [value for value, _, _ in items]
    offsets = tuple(offset for _, offset, _ in items)
    halves = tuple(half for _, _, half in items)
    n = len(items)
    first = total is None
    operands = [where, *lefts, *rights]
    in_specs = [pl.BlockSpec(memory_space=pltpu.SMEM)] + spaces(operands[1:], local)
    aliases = {}
    if not first:
        aliases = {len(operands): 0}
        operands.append(total)
        in_specs.append(pl.BlockSpec(memory_space=pltpu.VMEM))
    scratch = [
        pltpu.VMEM((n, CHUNK, BS), jnp.bfloat16),
        pltpu.VMEM((n, CHUNK, BS), jnp.bfloat16),
        pltpu.VMEM((2 * n, META, BS), jnp.bfloat16),
        pltpu.VMEM((2 * n, KB, BS), jnp.int32),
        pltpu.SMEM((2 * n, KB, BS), jnp.int32),
        pltpu.SemaphoreType.DMA((n,)),
        pltpu.SemaphoreType.DMA,
        pltpu.SemaphoreType.DMA,
    ]
    kernel = functools.partial(
        multiply_kernel, offsets, halves, first, grid_rows, grid_cols, len(rights)
    )
    return pl.pallas_call(
        kernel,
        out_shape=pltpu.VMEM((GR, KB, 2, BS, BS), jnp.float32),
        in_specs=in_specs,
        out_specs=pl.BlockSpec(memory_space=pltpu.VMEM),
        scratch_shapes=scratch,
        input_output_aliases=aliases,
        compiler_params=pltpu.CompilerParams(vmem_limit_bytes=16 * MIB),
    )(*operands)


def body(
    left_blocks,
    left_rows,
    left_count,
    left_level,
    right_blocks,
    right_cols,
    right_count,
    right_level,
):
    row, col = lax.axis_index("row"), lax.axis_index("col")
    grid_rows, grid_cols = lax.axis_size("row"), lax.axis_size("col")
    start = col + grid_cols - 1
    near = (((start + (row - start) % grid_rows) % grid_cols) // grid_rows).astype(jnp.int32)
    where = jnp.stack([row, col]).astype(jnp.int32)
    own = [pack_left(h, left_blocks, left_rows, left_count, left_level) for h in range(2)]
    right = (right_blocks, right_cols, right_count, right_level)
    held = [pack_right(which.reshape(1), *right) for which in (near, 1 - near)]

    hops = []
    up, down = list(own), list(own)
    for step in range(1, 4):
        for h in range(2):
            up[h] = shifted(up[h], "col", 1)
            down[h] = shifted(down[h], "col", -1)
        hops.append(
            [(up[0], -step, 0), (up[1], -step, 1), (down[0], step, 0), (down[1], step, 1)]
        )
    hops.append([(shifted(up[0], "col", 1), -4, 0), (shifted(down[1], "col", -1), 4, 1)])
    rights = []
    for s in range(2):
        partner = crossed(held[s], "row", 1)
        other = crossed(held[s], "row", 2)
        corner = crossed(other, "row", 1)
        rights += [held[s], partner, other, corner]

    local = own + held
    own_items = [(own[0], 0, 0), (own[1], 0, 1)]
    total = multiply(where, own_items + hops[0], rights[:4], None, local)
    total = multiply(where, hops[1], rights, total, local)
    last_right = fetch(where, 4, rights[4:], local)
    total = multiply(where, hops[2], rights[4:], total, local)
    early = flush(total)
    return finish(hops[3][0][0], hops[3][1][0], last_right, total, early)


def solution(mesh):
    in_specs = (
        P(("kpt", "row"), "col", None, None, None, None),
        P(("kpt", "row"), "col", None),
        P(("kpt", "row"), "col"),
        P(("kpt", "row"), "col", None),
        P("kpt", "row", "col", None, None, None, None),
        P("kpt", "row", "col", None),
        P("kpt", "row", "col"),
        P("kpt", "row", "col", None),
    )
    out_specs = P(("kpt", "row"), "col", None, None, None)

    return jax.shard_map(body, mesh=mesh, in_specs=in_specs, out_specs=out_specs, check_vma=False)
```

```python
import functools

import jax
import jax.numpy as jnp
from jax import lax
from jax.experimental import pallas as pl
from jax.experimental.pallas import tpu as pltpu
from jax.sharding import PartitionSpec as P

GR = 8
KB = 8
BS = 128
LEVEL_CUT = 7
HALF = 4
QUARTER = 2
BLOCK_ROWS = 2 * 2 * BS
META = 16
UNROLL = 4
MIB = 1024 * 1024
PACK_LIMIT = (60, 2)
CHUNK = HALF * BLOCK_ROWS
PANEL = KB * BLOCK_ROWS


def fill_table(table_ref, places, count, level):
    slot = lax.broadcasted_iota(jnp.int32, places.shape, 0)
    rows = (places, level, (slot < count).astype(jnp.int32))
    table = jnp.concatenate([row.astype(jnp.float32) for row in rows], axis=0)
    table = jnp.pad(table, ((0, META - table.shape[0]), (0, BS - table.shape[1])))
    table_ref[...] = table.astype(jnp.bfloat16)


def pack_left_kernel(
    half, rows_hbm, count_hbm, level_hbm, blocks_ref, out_ref, rows_ref, count_ref, level_ref, sem
):
    blocks = pltpu.make_async_copy(
        blocks_ref.at[pl.ds(half * CHUNK, CHUNK)], out_ref.at[pl.ds(0, CHUNK)], sem.at[3]
    )
    copies = [
        pltpu.make_async_copy(source, target, sem.at[i])
        for i, (source, target) in enumerate(
            ((rows_hbm, rows_ref), (count_hbm, count_ref), (level_hbm, level_ref))
        )
    ]
    blocks.start()
    for copy in copies:
        copy.start()
    for copy in copies:
        copy.wait()
    fill_table(out_ref.at[pl.ds(CHUNK, META)], rows_ref[...], count_ref[...], level_ref[...])
    blocks.wait()


def pack_left(half, blocks, rows, count, level):
    tables = (jnp.swapaxes(rows[0], 0, 1), count, jnp.swapaxes(level[0], 0, 1))
    return pl.pallas_call(
        functools.partial(pack_left_kernel, half),
        out_shape=pltpu.VMEM((CHUNK + META, BS), jnp.bfloat16),
        in_specs=[pl.BlockSpec(memory_space=pltpu.HBM)] * 4,
        out_specs=pl.BlockSpec(memory_space=pltpu.VMEM),
        scratch_shapes=[pltpu.VMEM(table.shape, jnp.int32) for table in tables]
        + [pltpu.SemaphoreType.DMA((4,))],
        compiler_params=pltpu.CompilerParams(vmem_limit_bytes=PACK_LIMIT[half] * MIB),
    )(*tables, blocks.reshape(-1, BS))


def pack_right_kernel(
    which_ref, cols_hbm, count_hbm, level_hbm, blocks_ref, out_ref,
    cols_ref, count_ref, level_ref, sem,
):
    which = which_ref[0]
    blocks = pltpu.make_async_copy(
        blocks_ref.at[which], out_ref.at[pl.ds(0, PANEL)], sem.at[3]
    )
    copies = [
        pltpu.make_async_copy(source.at[which], target, sem.at[i])
        for i, (source, target) in enumerate(
            ((cols_hbm, cols_ref), (count_hbm, count_ref), (level_hbm, level_ref))
        )
    ]
    blocks.start()
    for copy in copies:
        copy.start()
    for copy in copies:
        copy.wait()
    fill_table(out_ref.at[pl.ds(PANEL, META)], cols_ref[...], count_ref[...], level_ref[...])
    blocks.wait()


def pack_right(which, blocks, cols, count, level):
    tables = (
        jnp.swapaxes(cols[:, :, 0], 1, 2),
        jnp.swapaxes(count, 1, 2),
        jnp.swapaxes(level[:, :, 0], 1, 2),
    )
    return pl.pallas_call(
        pack_right_kernel,
        out_shape=pltpu.VMEM((PANEL + META, BS), jnp.bfloat16),
        in_specs=[pl.BlockSpec(memory_space=pltpu.SMEM)]
        + [pl.BlockSpec(memory_space=pltpu.HBM)] * 4,
        out_specs=pl.BlockSpec(memory_space=pltpu.VMEM),
        scratch_shapes=[pltpu.VMEM(table.shape[1:], jnp.int32) for table in tables]
        + [pltpu.SemaphoreType.DMA((4,))],
        compiler_params=pltpu.CompilerParams(vmem_limit_bytes=2 * MIB),
    )(which, *tables, blocks.reshape(-1, PANEL, BS))


def shifted(value, axis, steps):
    count = lax.axis_size(axis)
    return lax.ppermute(value, axis, [(i, (i + steps) % count) for i in range(count)])


def crossed(value, axis, bit):
    count = lax.axis_size(axis)
    return lax.ppermute(value, axis, [(i, i ^ bit) for i in range(count)])


def kept_pairs(table_smem, left_at, right_at, kb, m):
    level = table_smem[left_at, 2 + m, kb]
    live = table_smem[left_at, 4 + m, kb] > 0
    return [
        live
        & (table_smem[right_at, 4 + q, kb] > 0)
        & (level + table_smem[right_at, 2 + q, kb] >= LEVEL_CUT)
        for q in range(2)
    ]


def add_products(acc_ref, table_smem, left_at, right_at, kb, left_part, right_part):
    right = jnp.concatenate(
        [
            jnp.concatenate([right_part(0, 0), right_part(1, 0)], axis=1),
            jnp.concatenate([right_part(0, 1), right_part(1, 1)], axis=1),
        ],
        axis=0,
    )
    for m in range(2):
        row = table_smem[left_at, m, kb]
        kept = kept_pairs(table_smem, left_at, right_at, kb, m)
        real, imag = left_part(m, 0), left_part(m, 1)
        left = jnp.concatenate(
            [
                jnp.concatenate([real, -imag], axis=1),
                jnp.concatenate([imag, real], axis=1),
            ],
            axis=0,
        )
        product = jnp.dot(left, right, preferred_element_type=jnp.float32)
        for q in range(2):
            col = table_smem[right_at, q, kb]
            weight = kept[q].astype(jnp.float32)
            for part in range(2):
                acc_ref[row, col, part] += weight * product[
                    part * BS : (part + 1) * BS, q * BS : (q + 1) * BS
                ]


def tables_to_smem(table_buf, whole_buf, table_smem, sem):
    whole_buf[...] = table_buf[:, : whole_buf.shape[1]].astype(jnp.float32).astype(jnp.int32)
    to_smem = pltpu.make_async_copy(whole_buf, table_smem, sem)
    to_smem.start()
    to_smem.wait()


def right_source(where_ref, offset, grid_rows, grid_cols):
    panel = (where_ref[1] + offset + grid_cols) % grid_cols
    return (panel % grid_rows) ^ where_ref[0]


def multiply_kernel(offsets, halves, first, grid_rows, grid_cols, n_rights, *refs):
    n = len(offsets)
    where_ref = refs[0]
    lefts = refs[1 : 1 + n]
    rights = refs[1 + n : 1 + n + n_rights]
    acc_ref = refs[1 + n + n_rights + (not first)]
    left_buf, right_buf, table_buf, whole_buf, table_smem, data_sem, table_sem, smem_sem = refs[
        2 + n + n_rights + (not first) :
    ]

    def right_copies(i, act):
        source = right_source(where_ref, offsets[i], grid_rows, grid_cols)
        near = -1 <= offsets[i] <= grid_rows - 2
        for s in range(grid_rows):

            @pl.when(source == s)
            def _(s=s):
                act(rights[s if near else n_rights - grid_rows + s])

    for i in range(n):
        pltpu.make_async_copy(
            lefts[i].at[pl.ds(CHUNK, META)], table_buf.at[2 * i], table_sem
        ).start()
        right_copies(
            i,
            lambda src, i=i: pltpu.make_async_copy(
                src.at[pl.ds(PANEL, META)], table_buf.at[2 * i + 1], table_sem
            ).start(),
        )
    for i in range(n):
        pltpu.make_async_copy(lefts[i].at[pl.ds(0, CHUNK)], left_buf.at[i], data_sem.at[i]).start()
        right_copies(
            i,
            lambda src, i=i: pltpu.make_async_copy(
                src.at[pl.ds(halves[i] * CHUNK, CHUNK)], right_buf.at[i], data_sem.at[i]
            ).start(),
        )
    if first:
        acc_ref[...] = jnp.zeros_like(acc_ref)
    pltpu.make_async_copy(table_buf, table_buf, table_sem).wait()
    tables_to_smem(table_buf, whole_buf, table_smem, smem_sem)
    assert all(h == i % 2 for i, h in enumerate(halves))

    def one_item(i, carry):
        pltpu.make_async_copy(left_buf.at[i], left_buf.at[i], data_sem.at[i]).wait()
        pltpu.make_async_copy(right_buf.at[i], right_buf.at[i], data_sem.at[i]).wait()

        def one_kb(k, carry):
            base = pl.multiple_of(k * BLOCK_ROWS, BLOCK_ROWS)
            add_products(
                acc_ref,
                table_smem,
                2 * i,
                2 * i + 1,
                (i % 2) * HALF + k,
                lambda slot, part: left_buf[i, pl.ds(base + (2 * slot + part) * BS, BS), :],
                lambda slot, part: right_buf[i, pl.ds(base + (2 * slot + part) * BS, BS), :],
            )
            return carry

        return lax.fori_loop(0, HALF, one_kb, carry, unroll=UNROLL)

    lax.fori_loop(0, n, one_item, 0)


def fetch_kernel(offset, grid_rows, grid_cols, where_ref, *refs):
    *rights, out_ref, sem = refs
    source = right_source(where_ref, offset, grid_rows, grid_cols)
    for s in range(grid_rows):

        @pl.when(source == s)
        def _(s=s):
            pltpu.make_async_copy(rights[s], out_ref, sem).start()

    pltpu.make_async_copy(out_ref, out_ref, sem).wait()


def spaces(operands, local):
    return [
        pl.BlockSpec(memory_space=pltpu.VMEM if any(v is own for own in local) else pltpu.HBM)
        for v in operands
    ]


def fetch(where, offset, rights, local):
    kernel = functools.partial(
        fetch_kernel, offset, lax.axis_size("row"), lax.axis_size("col")
    )
    return pl.pallas_call(
        kernel,
        out_shape=pltpu.VMEM((PANEL + META, BS), jnp.bfloat16),
        in_specs=[pl.BlockSpec(memory_space=pltpu.SMEM)] + spaces(rights, local),
        out_specs=pl.BlockSpec(memory_space=pltpu.VMEM),
        scratch_shapes=[pltpu.SemaphoreType.DMA],
        compiler_params=pltpu.CompilerParams(vmem_limit_bytes=2 * MIB),
    )(where, *rights)


def flush_kernel(acc_ref, out_ref, stage_ref, sem):
    for r in range(GR):
        stage_ref[r] = acc_ref[r].astype(jnp.bfloat16)
        pltpu.make_async_copy(stage_ref.at[r], out_ref.at[r], sem).start()
    pltpu.make_async_copy(stage_ref, out_ref, sem).wait()


def flush(total):
    return pl.pallas_call(
        flush_kernel,
        out_shape=jax.ShapeDtypeStruct(total.shape, jnp.bfloat16),
        in_specs=[pl.BlockSpec(memory_space=pltpu.VMEM)],
        out_specs=pl.BlockSpec(memory_space=pltpu.HBM),
        scratch_shapes=[
            pltpu.VMEM(total.shape, jnp.bfloat16),
            pltpu.SemaphoreType.DMA,
        ],
        compiler_params=pltpu.CompilerParams(vmem_limit_bytes=6 * MIB),
    )(total)


def add_last(acc_ref, table_smem, lefts, right_ref, skipped):
    for h in range(2):

        def one_kb(k, carry, h=h):
            kb = h * HALF + skipped + k
            base = pl.multiple_of(k * BLOCK_ROWS, BLOCK_ROWS)
            add_products(
                acc_ref,
                table_smem,
                h,
                2,
                kb,
                lambda slot, part: lefts[h][pl.ds(base + (2 * slot + part) * BS, BS), :],
                lambda slot, part: right_ref[
                    pl.ds(kb * BLOCK_ROWS + (2 * slot + part) * BS, BS), :
                ],
            )
            return carry

        lax.fori_loop(0, QUARTER, one_kb, 0, unroll=QUARTER)


def load_tables(up_ref, down_ref, right_ref, table_buf):
    table_buf[0] = up_ref[pl.ds(QUARTER * BLOCK_ROWS, META), :]
    table_buf[1] = down_ref[pl.ds(QUARTER * BLOCK_ROWS, META), :]
    table_buf[2] = right_ref[pl.ds(PANEL, META), :]


def fourth_kernel(
    up_ref, down_ref, right_ref, total_ref, acc_ref, table_buf, whole_buf, table_smem, smem_sem
):
    load_tables(up_ref, down_ref, right_ref, table_buf)
    tables_to_smem(table_buf, whole_buf, table_smem, smem_sem)
    add_last(acc_ref, table_smem, (up_ref, down_ref), right_ref, HALF - QUARTER)


def fourth(up, down, right, total):
    return pl.pallas_call(
        fourth_kernel,
        out_shape=pltpu.VMEM(total.shape, jnp.float32),
        in_specs=[pl.BlockSpec(memory_space=pltpu.VMEM)] * 4,
        out_specs=pl.BlockSpec(memory_space=pltpu.VMEM),
        input_output_aliases={3: 0},
        scratch_shapes=[
            pltpu.VMEM((3, META, BS), jnp.bfloat16),
            pltpu.VMEM((3, KB, BS), jnp.int32),
            pltpu.SMEM((3, KB, BS), jnp.int32),
            pltpu.SemaphoreType.DMA,
        ],
        compiler_params=pltpu.CompilerParams(vmem_limit_bytes=5 * MIB),
    )(up, down, right, total)


def finish_kernel(
    up_ref, down_ref, early_up_ref, early_down_ref, right_ref, acc_ref, old_ref, out_ref,
    stage_ref, table_buf, whole_buf, table_smem, flag_smem, list_smem, out_sem, smem_sem,
):
    load_tables(early_up_ref, early_down_ref, right_ref, table_buf)
    for at in range(GR * KB):
        flag_smem[at] = 0
    list_smem[GR * KB] = 0
    tables_to_smem(table_buf, whole_buf, table_smem, smem_sem)

    def mark(kept, row, col):
        at = row * KB + col

        @pl.when(kept & (flag_smem[at] == 0))
        def _():
            flag_smem[at] = 1
            count = list_smem[GR * KB]
            list_smem[count] = at
            list_smem[GR * KB] = count + 1

    for h in range(2):
        for kb in range(h * HALF, h * HALF + QUARTER):
            for m in range(2):
                kept = kept_pairs(table_smem, h, 2, kb, m)
                for q in range(2):
                    mark(kept[q], table_smem[h, m, kb], table_smem[2, q, kb])

    add_last(acc_ref, table_smem, (up_ref, down_ref), right_ref, 0)

    count = list_smem[GR * KB]

    def write_block(i, carry):
        at = list_smem[i]
        row, col = at // KB, at % KB
        stage_ref[i] = acc_ref[row, col].astype(jnp.bfloat16)
        pltpu.make_async_copy(stage_ref.at[i], out_ref.at[row, col], out_sem.at[i]).start()
        return carry

    def wait_block(i, carry):
        pltpu.make_async_copy(stage_ref.at[i], out_ref.at[0, 0], out_sem.at[i]).wait()
        return carry

    lax.fori_loop(0, count, write_block, 0)
    lax.fori_loop(0, count, wait_block, 0)


def finish(late, early, right, total, old):
    most = 2 * QUARTER * 4
    return pl.pallas_call(
        finish_kernel,
        out_shape=jax.ShapeDtypeStruct(old.shape, old.dtype),
        in_specs=[pl.BlockSpec(memory_space=pltpu.VMEM)] * 6
        + [pl.BlockSpec(memory_space=pltpu.HBM)],
        out_specs=pl.BlockSpec(memory_space=pltpu.HBM),
        input_output_aliases={6: 0},
        scratch_shapes=[
            pltpu.VMEM((most, 2, BS, BS), jnp.bfloat16),
            pltpu.VMEM((3, META, BS), jnp.bfloat16),
            pltpu.VMEM((3, KB, BS), jnp.int32),
            pltpu.SMEM((3, KB, BS), jnp.int32),
            pltpu.SMEM((GR * KB,), jnp.int32),
            pltpu.SMEM((GR * KB + 1,), jnp.int32),
            pltpu.SemaphoreType.DMA((most,)),
            pltpu.SemaphoreType.DMA,
        ],
        compiler_params=pltpu.CompilerParams(vmem_limit_bytes=5 * MIB),
    )(*late, *early, right, total, old)


def multiply(where, items, rights, total, local):
    grid_rows = lax.axis_size("row")
    grid_cols = lax.axis_size("col")
    lefts = [value for value, _, _ in items]
    offsets = tuple(offset for _, offset, _ in items)
    halves = tuple(half for _, _, half in items)
    n = len(items)
    first = total is None
    operands = [where, *lefts, *rights]
    in_specs = [pl.BlockSpec(memory_space=pltpu.SMEM)] + spaces(operands[1:], local)
    aliases = {}
    if not first:
        aliases = {len(operands): 0}
        operands.append(total)
        in_specs.append(pl.BlockSpec(memory_space=pltpu.VMEM))
    scratch = [
        pltpu.VMEM((n, CHUNK, BS), jnp.bfloat16),
        pltpu.VMEM((n, CHUNK, BS), jnp.bfloat16),
        pltpu.VMEM((2 * n, META, BS), jnp.bfloat16),
        pltpu.VMEM((2 * n, KB, BS), jnp.int32),
        pltpu.SMEM((2 * n, KB, BS), jnp.int32),
        pltpu.SemaphoreType.DMA((n,)),
        pltpu.SemaphoreType.DMA,
        pltpu.SemaphoreType.DMA,
    ]
    kernel = functools.partial(
        multiply_kernel, offsets, halves, first, grid_rows, grid_cols, len(rights)
    )
    return pl.pallas_call(
        kernel,
        out_shape=pltpu.VMEM((GR, KB, 2, BS, BS), jnp.float32),
        in_specs=in_specs,
        out_specs=pl.BlockSpec(memory_space=pltpu.VMEM),
        scratch_shapes=scratch,
        input_output_aliases=aliases,
        compiler_params=pltpu.CompilerParams(vmem_limit_bytes=16 * MIB),
    )(*operands)


def body(
    left_blocks,
    left_rows,
    left_count,
    left_level,
    right_blocks,
    right_cols,
    right_count,
    right_level,
):
    row, col = lax.axis_index("row"), lax.axis_index("col")
    grid_rows, grid_cols = lax.axis_size("row"), lax.axis_size("col")
    start = col + grid_cols - 1
    near = (((start + (row - start) % grid_rows) % grid_cols) // grid_rows).astype(jnp.int32)
    where = jnp.stack([row, col]).astype(jnp.int32)
    own = [pack_left(h, left_blocks, left_rows, left_count, left_level) for h in range(2)]
    right = (right_blocks, right_cols, right_count, right_level)
    held = [pack_right(which.reshape(1), *right) for which in (near, 1 - near)]

    hops = []
    up, down = list(own), list(own)
    for step in range(1, 4):
        for h in range(2):
            up[h] = shifted(up[h], "col", 1)
            down[h] = shifted(down[h], "col", -1)
        hops.append(
            [(up[0], -step, 0), (up[1], -step, 1), (down[0], step, 0), (down[1], step, 1)]
        )
    cut = QUARTER * BLOCK_ROWS

    def part(value, begin, end):
        return value[begin:end]

    whole = CHUNK + META
    soon = (
        shifted(part(up[0], cut, whole), "col", 1), shifted(part(down[1], cut, whole), "col", -1)
    )
    late = (shifted(part(up[0], 0, cut), "col", 1), shifted(part(down[1], 0, cut), "col", -1))
    rights = []
    for s in range(2):
        partner = crossed(held[s], "row", 1)
        other = crossed(held[s], "row", 2)
        corner = crossed(other, "row", 1)
        rights += [held[s], partner, other, corner]

    local = own + held
    own_items = [(own[0], 0, 0), (own[1], 0, 1)]
    total = multiply(where, own_items + hops[0], rights[:4], None, local)
    total = multiply(where, hops[1], rights, total, local)
    last_right = fetch(where, 4, rights[4:], local)
    total = multiply(where, hops[2], rights[4:], total, local)
    total = fourth(*soon, last_right, total)
    early = flush(total)
    return finish(late, soon, last_right, total, early)


def solution(mesh):
    in_specs = (
        P(("kpt", "row"), "col", None, None, None, None),
        P(("kpt", "row"), "col", None),
        P(("kpt", "row"), "col"),
        P(("kpt", "row"), "col", None),
        P("kpt", "row", "col", None, None, None, None),
        P("kpt", "row", "col", None),
        P("kpt", "row", "col"),
        P("kpt", "row", "col", None),
    )
    out_specs = P(("kpt", "row"), "col", None, None, None)

    return jax.shard_map(body, mesh=mesh, in_specs=in_specs, out_specs=out_specs, check_vma=False)
```
